768 devices in a mesh: dp: 16 (over z_hi, y), ctx: 48 (over z_lo, x, core).
Axes of the slice: x: 4, y: 8, z: 12 (z_hi: 2, z_lo: 6; z = z_hi * 6 + z_lo), core: 2. Of those that a mesh axis runs over, the one named last changes fastest.
Arguments:
- queries: bfloat16 [48, 2048, 2560], P('ctx', 'dp'), may hold values from -20 to 20
- key_states: bfloat16 [48, 2048, 2560], P('ctx', 'dp'), may hold values from -20 to 20
- values: bfloat16 [48, 2048, 2560], P('ctx', 'dp'), may hold values from -6 to 6
- out_grad: bfloat16 [48, 2048, 2560], P('ctx', 'dp'), may hold values from -6 to 6
- block_links: int32 [2, 16], P(None, 'dp'), may hold values from -1 to 14, as said below
- sink_logit: float32 [20], replicated, may hold values from 4 to 8
Outputs:
- query_grad: bfloat16 [48, 2048, 2560], P('ctx', 'dp')
- key_grad: bfloat16 [48, 2048, 2560], P('ctx', 'dp')
- value_grad: bfloat16 [48, 2048, 2560], P('ctx', 'dp')
- sink_grad: float32 [20], replicated
The draws below stay inside these ranges and needn't reach their ends.
Inputs may be any that keep to these rules, and one draw needn't show every extreme that they name: block_links[j, b] is either -1 or b - 2**j; it is -1 wherever b - 2**j < 0; block_links[0, 15] is 14.
All inputs are finite; a program needn't handle non-finite values.
Results may differ from the reference program's by a relative error of at most 0.023.
Values may be sent and summed in bfloat16 or wider, within the bound.
A program may use at most 64 MiB of HBM per device.

```python
import jax
import jax.numpy as jnp
from jax import lax

H = 20
HEAD = 128
BLOCK = 128
LEVELS = 2
BATCH = 48
SEQ = 2048
NBLK = 16
BLK_DEV = 1


def draw_queries(key, part):
    own = jnp.clip(jax.random.normal(jax.random.fold_in(key, 31), (BATCH, SEQ, H * HEAD), jnp.float32), -4.0, 4.0)
    return own.astype(jnp.bfloat16)


def draw_key_states(key, part):
    own = jnp.clip(jax.random.normal(jax.random.fold_in(key, 32), (BATCH, SEQ, H * HEAD), jnp.float32), -4.0, 4.0)
    return own.astype(jnp.bfloat16)


def draw_block_links(key, part):
    block_ids = jnp.arange(NBLK, dtype=jnp.int32)[None, :]
    level_ids = jnp.arange(LEVELS, dtype=jnp.int32)[:, None]
    reach = (2 ** jnp.arange(LEVELS, dtype=jnp.int32))[:, None] * BLK_DEV
    target = block_ids - reach
    active = jax.random.randint(key, (LEVELS, NBLK), 0, 4) > 0
    forced = (level_ids == 0) & (block_ids == NBLK - 1)
    active = active | forced
    return jnp.where(active & (target >= 0), target, -1).astype(jnp.int32)


def shard_levels(rng, shape, split, smallest, high):
    level = 1.0
    for position, shards_of in split:
        steps = jax.random.uniform(jax.random.fold_in(jax.random.fold_in(rng, 6), position), (shards_of,), jnp.float32, smallest / len(split), high / len(split))
        level = level * jnp.repeat(jnp.exp(steps), shape[position] // shards_of).reshape((-1,) + (1,) * (len(shape) - 1 - position))
    return level


def noise(own_key, extent, scale, most, cuts=(), kind=jnp.bfloat16):
    values = jax.random.normal(own_key, extent, jnp.float32) * scale
    if len(cuts) > 0:
        values = shard_levels(own_key, extent, cuts, -0.22, 0.18) * values
    return jnp.clip(values, min=-most, max=most).astype(kind)


def setup_inputs(seed: int = 0) -> dict:
    arg_keys = jax.random.split(jax.random.key(seed), 7)
    queries = draw_queries(jax.random.fold_in(arg_keys[6], 71), 0)
    key_states = draw_key_states(jax.random.fold_in(arg_keys[6], 71), 0)
    values = noise(arg_keys[2], (BATCH, SEQ, H * HEAD), 1.0, 6.0, ((0, 48), (1, 16)))
    out_grad = noise(arg_keys[3], (BATCH, SEQ, H * HEAD), 1.0, 6.0, ((0, 48), (1, 16)))
    block_links = draw_block_links(jax.random.fold_in(arg_keys[6], 71), 0)
    sink_logit = jnp.clip(jax.random.uniform(arg_keys[5], (H,), jnp.float32, 4.0, 8.0), 4.0, 8.0)
    return {"queries": queries, "key_states": key_states, "values": values, "out_grad": out_grad, "block_links": block_links, "sink_logit": sink_logit}


NEG_FILL = -1.0e30


def causal_table(block_len):
    rows_iota = lax.broadcasted_iota(jnp.int32, (block_len, block_len), 0)
    cols_iota = lax.broadcasted_iota(jnp.int32, (block_len, block_len), 1)
    return rows_iota >= cols_iota


def reference(queries, key_states, values, out_grad, block_links, sink_logit):
    score_scale = HEAD ** -0.5
    valid_link = block_links >= 0
    safe_link = jnp.maximum(block_links, 0).astype(jnp.int32)
    causal = jnp.broadcast_to(causal_table(BLOCK), (NBLK, BLOCK, BLOCK))
    remote_masks = [jnp.broadcast_to(valid_link[level_num][:, None, None], (NBLK, BLOCK, BLOCK)) for level_num in range(LEVELS)]
    allowed = jnp.concatenate([causal] + remote_masks, axis=2)

    def one_sequence(item):
        q_seq, k_seq, v_seq, g_seq = item
        q_blocks = q_seq.reshape(NBLK, BLOCK, H, HEAD).astype(jnp.float32)
        k_blocks = k_seq.reshape(NBLK, BLOCK, H, HEAD).astype(jnp.float32)
        v_blocks = v_seq.reshape(NBLK, BLOCK, H, HEAD).astype(jnp.float32)
        g_blocks = g_seq.reshape(NBLK, BLOCK, H, HEAD).astype(jnp.float32)
        key_all = jnp.concatenate([k_blocks] + [k_blocks[safe_link[level_num]] for level_num in range(LEVELS)], axis=1)
        val_all = jnp.concatenate([v_blocks] + [v_blocks[safe_link[level_num]] for level_num in range(LEVELS)], axis=1)
        scores = jnp.einsum("bqhd,bkhd->bhqk", q_blocks, key_all) * score_scale
        scores = jnp.where(allowed[:, None], scores, NEG_FILL)
        row_max = jnp.maximum(jnp.max(scores, axis=-1), sink_logit[None, :, None])
        exp_scores = jnp.exp(scores - row_max[..., None])
        sink_exp = jnp.exp(sink_logit[None, :, None] - row_max)
        denominator = jnp.sum(exp_scores, axis=-1) + sink_exp
        soft_prob = exp_scores / denominator[..., None]
        sink_prob = sink_exp / denominator
        weights = lax.optimization_barrier(soft_prob.astype(jnp.bfloat16)).astype(jnp.float32)
        output = jnp.einsum("bhqk,bkhd->bqhd", weights, val_all).astype(jnp.bfloat16)
        output_wide = lax.optimization_barrier(output).astype(jnp.float32)
        row_delta = jnp.transpose(jnp.sum(g_blocks * output_wide, axis=-1), (0, 2, 1))
        prob_grad = jnp.einsum("bqhd,bkhd->bhqk", g_blocks, val_all)
        score_grad = (soft_prob * (prob_grad - row_delta[..., None])).astype(jnp.bfloat16)
        score_grad = lax.optimization_barrier(score_grad).astype(jnp.float32)
        query_grad = (jnp.einsum("bhqk,bkhd->bqhd", score_grad, key_all) * score_scale).astype(jnp.bfloat16)
        key_terms = jnp.einsum("bhqk,bqhd->bkhd", score_grad, q_blocks) * score_scale
        value_terms = jnp.einsum("bhqk,bqhd->bkhd", weights, g_blocks)
        key_grad = key_terms[:, :BLOCK]
        value_grad = value_terms[:, :BLOCK]
        for level_num in range(LEVELS):
            first_col = BLOCK * (1 + level_num)
            key_part = lax.optimization_barrier(key_terms[:, first_col:first_col + BLOCK].astype(jnp.bfloat16)).astype(jnp.float32)
            value_part = lax.optimization_barrier(value_terms[:, first_col:first_col + BLOCK].astype(jnp.bfloat16)).astype(jnp.float32)
            key_grad = key_grad.at[safe_link[level_num]].add(key_part)
            value_grad = value_grad.at[safe_link[level_num]].add(value_part)
        sink_term = -jnp.sum(sink_prob * row_delta, axis=(0, 2))
        return (query_grad.reshape(SEQ, H * HEAD),
                key_grad.astype(jnp.bfloat16).reshape(SEQ, H * HEAD),
                value_grad.astype(jnp.bfloat16).reshape(SEQ, H * HEAD),
                sink_term)

    grads = lax.map(one_sequence, (queries, key_states, values, out_grad))
    return (grads[0], grads[1], grads[2], jnp.sum(grads[3], axis=0))
```

```python
import functools

import jax
import jax.numpy as jnp
from jax import lax
from jax.experimental import pallas as pl
from jax.experimental.pallas import tpu as pltpu
from jax.sharding import PartitionSpec as P

MESH = pl.DeviceIdType.MESH
BLOCK = 128
HEAD = 128
CHUNKS = 10
AHEAD = 2
NEG_FILL = -1e30
CORES = 2


def body_kernel(
    dims,
    links,
    sink,
    q_ref,
    k_ref,
    v_ref,
    g_ref,
    dq_ref,
    dk_ref,
    dv_ref,
    sg_ref,
    kv1,
    kv2,
    rt1,
    rs0,
    st1,
    ss0,
    near,
    own,
    sink_rows,
    plane,
    column,
    row,
    up_send,
    up_recv,
    fw_send,
    fw_recv,
    t1_send,
    t1_recv,
    s0_send,
    s0_recv,
    re_send,
    plane_sem,
    column_sem,
    row_sem,
):
    n, n_ctx, heads = dims
    chunks = CHUNKS
    per = heads // chunks
    width = per * HEAD
    half = n // 2
    scale = HEAD**-0.5
    me = lax.axis_index("dp")
    ctx = lax.axis_index("ctx")
    last = n - 1
    is_lo = me == half - 1
    is_hi = me == half
    is_relay = (me == 0) | (me == last)
    relay_par = jnp.where(me == 0, 1, 0)

    n_plane = 8
    n_zlo = n_ctx // n_plane
    n_col = 2 * n_zlo
    pos_plane = lax.rem(ctx, n_plane)
    zlo = ctx // n_plane
    zhi = me // half
    y = lax.rem(me, half)
    pos_col = zhi * n_zlo + zlo

    def plane_peer(slot):
        return {"dp": me, "ctx": zlo * n_plane + slot}

    def column_peer(slot):
        return {
            "dp": (slot // n_zlo) * half + y,
            "ctx": lax.rem(slot, n_zlo) * n_plane + pos_plane,
        }

    def row_peer(slot):
        return {"dp": zhi * half + slot, "ctx": ctx}

    groups = (
        (n_plane, pos_plane, plane_peer, plane, plane_sem),
        (n_col, pos_col, column_peer, column, column_sem),
        (half, y, row_peer, row, row_sem),
    )

    barrier = pltpu.get_barrier_semaphore()
    total = 0
    for size, pos, peer, _, _ in groups:

        def greet(step, carry, size=size, pos=pos, peer=peer):
            pl.semaphore_signal(
                barrier, inc=1, device_id=peer(lax.rem(pos + step, size)), device_id_type=MESH
            )
            return carry

        lax.fori_loop(1, size, greet, 0)
        total += size - 1
    pl.semaphore_wait(barrier, total)

    def relay_of(c):
        return jnp.where(lax.rem(c, 2) == 0, last, 0)

    def up_device(c):
        return {"dp": jnp.where(is_lo, relay_of(c), jnp.minimum(me + 1, last)), "ctx": ctx}

    def down_device(c):
        return {"dp": jnp.where(is_hi, relay_of(c), jnp.maximum(me - 1, 0)), "ctx": ctx}

    def up_slot(c):
        return c + jnp.where(is_lo, chunks, 0)

    def down_slot(c):
        return c + jnp.where(is_hi, chunks, 0)

    def lanes(c):
        return pl.ds(pl.multiple_of(c * width, width), width)

    def copy(src, dst, send, recv, device):
        return pltpu.make_async_remote_copy(
            src_ref=src,
            dst_ref=dst,
            send_sem=send,
            recv_sem=recv,
            device_id=device,
            device_id_type=MESH,
        )

    def own_copies(c):
        slot = up_slot(c)
        return [
            copy(
                ref.at[:, lanes(c)],
                kv1.at[slot, which],
                up_send.at[c],
                up_recv.at[slot],
                up_device(c),
            )
            for which, ref in enumerate((k_ref, v_ref))
        ]

    def send_own(c):
        for each in own_copies(c):
            each.start()

    def fw_copy(c):
        slot = up_slot(c)
        return copy(kv1.at[c], kv2.at[slot], fw_send.at[c], fw_recv.at[slot], up_device(c))

    def t1_copy(c):
        slot = down_slot(c)
        return copy(st1.at[c], rt1.at[slot], t1_send.at[c], t1_recv.at[slot], down_device(c))

    def s0_copy(c):
        slot = down_slot(c)
        return copy(ss0.at[c], rs0.at[slot], s0_send.at[c], s0_recv.at[slot], down_device(c))

    def landed(ref, sem, slot):
        pltpu.make_async_copy(ref.at[slot], ref.at[slot], sem.at[slot]).wait()

    relays = (
        (kv1, up_recv, half),
        (kv2, fw_recv, half),
        (rt1, t1_recv, half - 1),
        (rs0, s0_recv, half - 1),
    )

    def relay_copy(which, c):
        ref, sem, target = relays[which]
        return copy(
            ref.at[chunks + c],
            ref.at[c],
            re_send.at[which, c],
            sem.at[c],
            {"dp": target, "ctx": ctx},
        )

    def relay(which, c):
        @pl.when(is_relay & (lax.rem(c, 2) == relay_par) & (c >= 0) & (c < chunks))
        def _():
            ref, sem, _ = relays[which]
            landed(ref, sem, chunks + c)
            relay_copy(which, c).start()

    has_down = me >= 1
    has_far = me >= 2
    has_up = me <= last - 1

    @pl.when(has_up)
    def _():
        for c in range(AHEAD):
            send_own(jnp.int32(c))

    zero = jnp.zeros((2, BLOCK, width), jnp.bfloat16)

    def clear(ref):
        def one(c, carry):
            ref[c] = zero
            return carry

        lax.fori_loop(0, chunks, one, 0)

    @pl.when(me == 0)
    def _():
        clear(kv1)

    @pl.when(me <= 1)
    def _():
        clear(kv2)

    @pl.when(me == last)
    def _():
        clear(rs0)
        clear(rt1)

    sink_rows[...] = jnp.zeros_like(sink_rows)
    bias = [jnp.where(links[level, 0] >= 0, 0.0, NEG_FILL) for level in range(2)]
    key_pos = lax.broadcasted_iota(jnp.int32, (BLOCK, BLOCK), 0)
    query_pos = lax.broadcasted_iota(jnp.int32, (BLOCK, BLOCK), 1)
    causal = query_pos >= key_pos

    def dot(a, b, dims):
        return lax.dot_general(a, b, (dims, ((), ())), preferred_element_type=jnp.float32)

    def attend(c):
        for i in range(per):
            head = c * per + i
            at = pl.ds(pl.multiple_of(c * width + i * HEAD, HEAD), HEAD)
            part = slice(i * HEAD, (i + 1) * HEAD)
            q = q_ref[:, at]
            g = g_ref[:, at]
            keys = (k_ref[:, at], kv1[c, 0, :, part], kv2[c, 0, :, part])
            vals = (v_ref[:, at], kv1[c, 1, :, part], kv2[c, 1, :, part])
            logit = sink[head]
            scores = [dot(k, q, ((1,), (1,))) * scale for k in keys]
            scores = [
                jnp.where(causal, scores[0], NEG_FILL),
                scores[1] + bias[0],
                scores[2] + bias[1],
            ]
            top = jnp.maximum(jnp.maximum(scores[0], scores[1]), scores[2])
            top = jnp.maximum(jnp.max(top, axis=0, keepdims=True), logit)
            exps = [jnp.exp(s - top) for s in scores]
            sink_exp = jnp.exp(logit - top)
            denom = jnp.sum(exps[0] + exps[1] + exps[2], axis=0, keepdims=True) + sink_exp
            inverse = 1.0 / denom
            probs = [e * inverse for e in exps]
            prob_grads = [dot(v, g, ((1,), (1,))) for v in vals]
            mixed = (
                probs[0] * prob_grads[0] + probs[1] * prob_grads[1] + probs[2] * prob_grads[2]
            )
            delta = jnp.sum(mixed, axis=0, keepdims=True)
            score_grads = [
                (p * (d - delta)).astype(jnp.bfloat16) for p, d in zip(probs, prob_grads)
            ]
            weights = [p.astype(jnp.bfloat16) for p in probs]
            sink_rows[pl.ds(head, 1), :] = -(sink_exp * inverse * delta)
            dq = dot(score_grads[0], keys[0], ((0,), (0,)))
            dq += dot(score_grads[1], keys[1], ((0,), (0,)))
            dq += dot(score_grads[2], keys[2], ((0,), (0,)))
            dq_ref[:, at] = (dq * scale).astype(jnp.bfloat16)
            own[c, 0, :, part] = dot(score_grads[0], q, ((1,), (0,))) * scale
            own[c, 1, :, part] = dot(weights[0], g, ((1,), (0,)))
            near[c, 0, :, part] = dot(score_grads[1], q, ((1,), (0,))) * scale
            near[c, 1, :, part] = dot(weights[1], g, ((1,), (0,)))
            st1[c, 0, :, part] = (dot(score_grads[2], q, ((1,), (0,))) * scale).astype(
                jnp.bfloat16
            )
            st1[c, 1, :, part] = dot(weights[2], g, ((1,), (0,))).astype(jnp.bfloat16)

    def pass_near(c):
        @pl.when(has_down & has_up)
        def _():
            landed(rt1, t1_recv, c)

        @pl.when(has_down)
        def _():
            ss0[c] = (near[c] + rt1[c].astype(jnp.float32)).astype(jnp.bfloat16)
            s0_copy(c).start()

    def finish(c):
        @pl.when(has_up)
        def _():
            landed(rs0, s0_recv, c)

        dk_ref[:, lanes(c)] = (own[c, 0] + rs0[c, 0].astype(jnp.float32)).astype(jnp.bfloat16)
        dv_ref[:, lanes(c)] = (own[c, 1] + rs0[c, 1].astype(jnp.float32)).astype(jnp.bfloat16)

    def step(c, carry):
        relay(0, c)

        @pl.when(has_down)
        def _():
            landed(kv1, up_recv, c)

        @pl.when(has_down & has_up)
        def _():
            fw_copy(c).start()

        @pl.when(has_up & (c + AHEAD < chunks))
        def _():
            send_own(c + AHEAD)

        relay(1, c)
        relay(2, c - 1)

        @pl.when(has_far)
        def _():
            landed(kv2, fw_recv, c)

        attend(c)

        @pl.when(has_far)
        def _():
            t1_copy(c).start()

        relay(3, c - 2)

        @pl.when(c >= 1)
        def _():
            pass_near(c - 1)

        @pl.when(c >= 3)
        def _():
            finish(c - 3)

        return carry

    lax.fori_loop(0, chunks, step, 0)

    def publish(which, value):
        size, pos, peer, buf, sem = groups[which]
        buf[pos] = value

        def one(s, carry):
            slot = lax.rem(pos + s, size)
            copy(buf.at[pos], buf.at[pos], sem.at[0, s], sem.at[1, pos], peer(slot)).start()
            return carry

        lax.fori_loop(1, size, one, 0)

    def collect(which):
        size, pos, peer, buf, sem = groups[which]

        def one(s, carry):
            slot = lax.rem(pos + s, size)
            pltpu.make_async_copy(buf.at[slot], buf.at[slot], sem.at[1, slot]).wait()
            pltpu.make_async_copy(buf.at[pos], buf.at[pos], sem.at[0, s]).wait()
            return carry

        lax.fori_loop(1, size, one, 0)
        out = buf[0]
        for s in range(1, size):
            out = out + buf[s]
        return out

    by_lane = jnp.sum(jnp.transpose(sink_rows[...]), axis=0, keepdims=True)
    publish(0, jnp.broadcast_to(by_lane, (8, 128)))
    relay(2, jnp.int32(chunks - 1))
    pass_near(jnp.int32(chunks - 1))
    publish(1, collect(0))
    relay(3, jnp.int32(chunks - 2))
    relay(3, jnp.int32(chunks - 1))
    finish(jnp.int32(chunks - 3))
    finish(jnp.int32(chunks - 2))
    publish(2, collect(1))
    finish(jnp.int32(chunks - 1))
    sg_ref[...] = collect(2)

    def drain(c, carry):
        @pl.when(has_up)
        def _():
            pltpu.make_async_copy(kv1.at[0], kv1.at[0], up_send.at[c]).wait()

        @pl.when(has_up & has_down)
        def _():
            pltpu.make_async_copy(kv1.at[0], kv1.at[0], fw_send.at[c]).wait()

        @pl.when(has_far)
        def _():
            pltpu.make_async_copy(st1.at[0], st1.at[0], t1_send.at[c]).wait()

        @pl.when(has_down)
        def _():
            pltpu.make_async_copy(ss0.at[0], ss0.at[0], s0_send.at[c]).wait()

        @pl.when(is_relay & (lax.rem(c, 2) == relay_par))
        def _():
            for which in range(4):
                pltpu.make_async_copy(kv1.at[0], kv1.at[0], re_send.at[which, c]).wait()

        return carry

    lax.fori_loop(0, chunks, drain, 0)


def solution(mesh):
    n, n_ctx = mesh.shape["dp"], mesh.shape["ctx"]

    def body(queries, key_states, values, out_grad, block_links, sink_logit):
        shape = queries.shape
        tokens, full = shape[1], shape[2]
        heads = sink_logit.shape[0]
        width = full // CHUNKS
        flat = [a.reshape(tokens, full) for a in (queries, key_states, values, out_grad)]
        vmem = pl.BlockSpec(memory_space=pltpu.VMEM)
        smem = pl.BlockSpec(memory_space=pltpu.SMEM)
        wide = pltpu.VMEM((2 * CHUNKS, 2, BLOCK, width), jnp.bfloat16)
        once = pltpu.VMEM((CHUNKS, 2, BLOCK, width), jnp.bfloat16)
        sums = pltpu.VMEM((CHUNKS, 2, BLOCK, width), jnp.float32)
        dma = pltpu.SemaphoreType.DMA
        n_col = 2 * (n_ctx // 8)
        dq, dk, dv, sg = pl.pallas_call(
            functools.partial(body_kernel, (n, n_ctx, heads)),
            out_shape=[jax.ShapeDtypeStruct((tokens, full), jnp.bfloat16)] * 3
            + [jax.ShapeDtypeStruct((8, 128), jnp.float32)],
            in_specs=[smem, smem] + [vmem] * 4,
            out_specs=[vmem] * 4,
            scratch_shapes=[
                wide,
                wide,
                wide,
                wide,
                once,
                once,
                sums,
                sums,
                pltpu.VMEM((128, 128), jnp.float32),
                pltpu.VMEM((8, 8, 128), jnp.float32),
                pltpu.VMEM((n_col, 8, 128), jnp.float32),
                pltpu.VMEM((n // 2, 8, 128), jnp.float32),
                dma((CHUNKS,)),
                dma((2 * CHUNKS,)),
                dma((CHUNKS,)),
                dma((2 * CHUNKS,)),
                dma((CHUNKS,)),
                dma((2 * CHUNKS,)),
                dma((CHUNKS,)),
                dma((2 * CHUNKS,)),
                dma((4, CHUNKS)),
                dma((2, 8)),
                dma((2, n_col)),
                dma((2, n // 2)),
            ],
            compiler_params=pltpu.CompilerParams(
                collective_id=0, has_side_effects=True, vmem_limit_bytes=50 * 1024 * 1024
            ),
        )(block_links, sink_logit, *flat)
        return dq.reshape(shape), dk.reshape(shape), dv.reshape(shape), sg[0, :heads]

    placed = (
        P("ctx", "dp", None),
        P("ctx", "dp", None),
        P("ctx", "dp", None),
        P("ctx", "dp", None),
        P(None, "dp"),
        P(),
    )
    return jax.shard_map(
        body,
        mesh=mesh,
        in_specs=placed,
        out_specs=(P("ctx", "dp", None), P("ctx", "dp", None), P("ctx", "dp", None), P()),
        check_vma=False,
    )
```

```python
import functools

import jax
import jax.numpy as jnp
from jax import lax
from jax.experimental import pallas as pl
from jax.experimental.pallas import tpu as pltpu
from jax.sharding import PartitionSpec as P

MESH = pl.DeviceIdType.MESH
BLOCK = 128
HEAD = 128
CHUNKS = 10
AHEAD = 2
NEG_FILL = -1e30
LAG_LO = 5
LAG_T1 = 3
LAG_S0 = 4
LAG_END = 6


def body_kernel(
    dims,
    links,
    sink,
    q_ref,
    k_ref,
    v_ref,
    g_ref,
    dq_ref,
    dk_ref,
    dv_ref,
    sg_ref,
    kv1,
    kv2,
    rt1,
    rs0,
    st1,
    ss0,
    near,
    own,
    sink_rows,
    plane,
    column,
    row,
    up_send,
    up_recv,
    fw_send,
    fw_recv,
    t1_send,
    t1_recv,
    s0_send,
    s0_recv,
    re_send,
    plane_sem,
    column_sem,
    row_sem,
):
    n, n_ctx, heads = dims
    chunks = CHUNKS
    per = heads // chunks
    width = per * HEAD
    half = n // 2
    scale = HEAD**-0.5
    me = lax.axis_index("dp")
    ctx = lax.axis_index("ctx")
    last = n - 1
    is_lo = me == half - 1
    is_hi = me == half
    is_relay = (me == 0) | (me == last)
    relay_half = jnp.where(me == 0, 1, 0)

    n_plane = 8
    n_zlo = n_ctx // n_plane
    n_col = 2 * n_zlo
    pos_plane = lax.rem(ctx, n_plane)
    zlo = ctx // n_plane
    zhi = me // half
    y = lax.rem(me, half)
    across = lax.rem(zlo + n_zlo // 2, n_zlo) * n_plane + pos_plane
    pos_col = zhi * n_zlo + zlo

    def plane_peer(slot):
        return {"dp": me, "ctx": zlo * n_plane + slot}

    def column_peer(slot):
        return {
            "dp": (slot // n_zlo) * half + y,
            "ctx": lax.rem(slot, n_zlo) * n_plane + pos_plane,
        }

    def row_peer(slot):
        return {"dp": zhi * half + slot, "ctx": ctx}

    groups = (
        (n_plane, pos_plane, plane_peer, plane, plane_sem),
        (n_col, pos_col, column_peer, column, column_sem),
        (half, y, row_peer, row, row_sem),
    )

    barrier = pltpu.get_barrier_semaphore()
    total = 0
    for size, pos, peer, _, _ in groups:

        def greet(step, carry, size=size, pos=pos, peer=peer):
            pl.semaphore_signal(
                barrier, inc=1, device_id=peer(lax.rem(pos + step, size)), device_id_type=MESH
            )
            return carry

        lax.fori_loop(1, size, greet, 0)
        total += size - 1
    is_edge = is_lo | is_hi | is_relay

    @pl.when(is_edge)
    def _():
        facing = jnp.where(me < half, half - 1 - me, half + last - me)
        pl.semaphore_signal(
            barrier, inc=1, device_id={"dp": facing, "ctx": across}, device_id_type=MESH
        )

    pl.semaphore_wait(barrier, total + jnp.where(is_edge, 1, 0))

    def up_device(which):
        relay_dp = last if which == 0 else 0
        return {
            "dp": jnp.where(is_lo, relay_dp, jnp.minimum(me + 1, last)),
            "ctx": jnp.where(is_lo, across, ctx),
        }

    def down_device(which):
        relay_dp = last if which == 0 else 0
        return {
            "dp": jnp.where(is_hi, relay_dp, jnp.maximum(me - 1, 0)),
            "ctx": jnp.where(is_hi, across, ctx),
        }

    def up_slot(c):
        return c + jnp.where(is_lo, chunks, 0)

    def down_slot(c):
        return c + jnp.where(is_hi, chunks, 0)

    def lanes(c):
        return pl.ds(pl.multiple_of(c * width, width), width)

    def copy(src, dst, send, recv, device):
        return pltpu.make_async_remote_copy(
            src_ref=src,
            dst_ref=dst,
            send_sem=send,
            recv_sem=recv,
            device_id=device,
            device_id_type=MESH,
        )

    def own_copies(c):
        slot = up_slot(c)
        return [
            copy(
                ref.at[:, lanes(c)],
                kv1.at[slot, which],
                up_send.at[c],
                up_recv.at[slot],
                up_device(which),
            )
            for which, ref in enumerate((k_ref, v_ref))
        ]

    def send_own(c):
        for each in own_copies(c):
            each.start()

    def pair(src, dst, send, recv, c, slot, device):
        for which in range(2):
            copy(
                src.at[c, which], dst.at[slot, which], send.at[c], recv.at[slot], device(which)
            ).start()

    def send_fw(c):
        pair(kv1, kv2, fw_send, fw_recv, c, up_slot(c), up_device)

    def send_t1(c):
        pair(st1, rt1, t1_send, t1_recv, c, down_slot(c), down_device)

    def send_s0(c):
        pair(ss0, rs0, s0_send, s0_recv, c, down_slot(c), down_device)

    def landed(ref, sem, slot):
        pltpu.make_async_copy(ref.at[slot], ref.at[slot], sem.at[slot]).wait()

    relays = (
        (kv1, up_recv, half),
        (kv2, fw_recv, half),
        (rt1, t1_recv, half - 1),
        (rs0, s0_recv, half - 1),
    )

    def relay(stream, c):
        @pl.when(is_relay & (c >= 0) & (c < chunks))
        def _():
            ref, sem, target = relays[stream]
            held = ref.at[chunks + c, relay_half]
            pltpu.make_async_copy(held, held, sem.at[chunks + c]).wait()
            copy(
                held,
                ref.at[c, relay_half],
                re_send.at[stream, c],
                sem.at[c],
                {"dp": target, "ctx": across},
            ).start()

    has_down = me >= 1
    has_far = me >= 2
    has_up = me <= last - 1

    @pl.when(has_up)
    def _():
        for c in range(AHEAD + 1):
            send_own(jnp.int32(c))

    zero = jnp.zeros((2, BLOCK, width), jnp.bfloat16)

    def clear(ref):
        def one(c, carry):
            ref[c] = zero
            return carry

        lax.fori_loop(0, chunks, one, 0)

    @pl.when(me == 0)
    def _():
        clear(kv1)

    @pl.when(me <= 1)
    def _():
        clear(kv2)

    @pl.when(me == last)
    def _():
        clear(rs0)
        clear(rt1)

    sink_rows[...] = jnp.zeros_like(sink_rows)
    bias = [jnp.where(links[level, 0] >= 0, 0.0, NEG_FILL) for level in range(2)]
    key_pos = lax.broadcasted_iota(jnp.int32, (BLOCK, BLOCK), 0)
    query_pos = lax.broadcasted_iota(jnp.int32, (BLOCK, BLOCK), 1)
    causal = query_pos >= key_pos

    def dot(a, b, dims):
        return lax.dot_general(a, b, (dims, ((), ())), preferred_element_type=jnp.float32)

    def attend(c):
        for i in range(per):
            head = c * per + i
            at = pl.ds(pl.multiple_of(c * width + i * HEAD, HEAD), HEAD)
            part = slice(i * HEAD, (i + 1) * HEAD)
            q = q_ref[:, at]
            g = g_ref[:, at]
            keys = (k_ref[:, at], kv1[c, 0, :, part], kv2[c, 0, :, part])
            vals = (v_ref[:, at], kv1[c, 1, :, part], kv2[c, 1, :, part])
            logit = sink[head]
            scores = [dot(k, q, ((1,), (1,))) * scale for k in keys]
            scores = [
                jnp.where(causal, scores[0], NEG_FILL),
                scores[1] + bias[0],
                scores[2] + bias[1],
            ]
            top = jnp.maximum(jnp.maximum(scores[0], scores[1]), scores[2])
            top = jnp.maximum(jnp.max(top, axis=0, keepdims=True), logit)
            exps = [jnp.exp(s - top) for s in scores]
            sink_exp = jnp.exp(logit - top)
            denom = jnp.sum(exps[0] + exps[1] + exps[2], axis=0, keepdims=True) + sink_exp
            inverse = 1.0 / denom
            probs = [e * inverse for e in exps]
            prob_grads = [dot(v, g, ((1,), (1,))) for v in vals]
            mixed = (
                probs[0] * prob_grads[0] + probs[1] * prob_grads[1] + probs[2] * prob_grads[2]
            )
            delta = jnp.sum(mixed, axis=0, keepdims=True)
            score_grads = [
                (p * (d - delta)).astype(jnp.bfloat16) for p, d in zip(probs, prob_grads)
            ]
            weights = [p.astype(jnp.bfloat16) for p in probs]
            sink_rows[pl.ds(head, 1), :] = -(sink_exp * inverse * delta)
            dq = dot(score_grads[0], keys[0], ((0,), (0,)))
            dq += dot(score_grads[1], keys[1], ((0,), (0,)))
            dq += dot(score_grads[2], keys[2], ((0,), (0,)))
            dq_ref[:, at] = (dq * scale).astype(jnp.bfloat16)
            own[c, 0, :, part] = dot(score_grads[0], q, ((1,), (0,))) * scale
            own[c, 1, :, part] = dot(weights[0], g, ((1,), (0,)))
            near[c, 0, :, part] = dot(score_grads[1], q, ((1,), (0,))) * scale
            near[c, 1, :, part] = dot(weights[1], g, ((1,), (0,)))
            st1[c, 0, :, part] = (dot(score_grads[2], q, ((1,), (0,))) * scale).astype(
                jnp.bfloat16
            )
            st1[c, 1, :, part] = dot(weights[2], g, ((1,), (0,))).astype(jnp.bfloat16)

    def pass_near(c):
        @pl.when(has_down & has_up)
        def _():
            landed(rt1, t1_recv, c)

        @pl.when(has_down)
        def _():
            ss0[c] = (near[c] + rt1[c].astype(jnp.float32)).astype(jnp.bfloat16)
            send_s0(c)

    def finish(c):
        @pl.when(has_up)
        def _():
            landed(rs0, s0_recv, c)

        dk_ref[:, lanes(c)] = (own[c, 0] + rs0[c, 0].astype(jnp.float32)).astype(jnp.bfloat16)
        dv_ref[:, lanes(c)] = (own[c, 1] + rs0[c, 1].astype(jnp.float32)).astype(jnp.bfloat16)

    def forward(c):
        @pl.when(has_down & (c < chunks))
        def _():
            landed(kv1, up_recv, c)

        @pl.when(has_down & has_up & (c < chunks))
        def _():
            send_fw(c)

    lag = jnp.where(is_lo, LAG_LO, 1)

    def near_lagged(c):
        @pl.when((c >= lag) & (c - lag < chunks))
        def _():
            pass_near(c - lag)

    def step(c, carry):
        relay(0, c + 1)
        forward(c + 1)

        @pl.when(has_up & (c + AHEAD + 1 < chunks))
        def _():
            send_own(c + AHEAD + 1)

        relay(1, c)

        @pl.when(has_far)
        def _():
            landed(kv2, fw_recv, c)

        attend(c)

        @pl.when(has_far)
        def _():
            send_t1(c)

        relay(2, c - LAG_T1)
        near_lagged(c)
        relay(3, c - LAG_S0)

        @pl.when(c >= LAG_END)
        def _():
            finish(c - LAG_END)

        return carry

    relay(0, jnp.int32(0))
    forward(jnp.int32(0))
    lax.fori_loop(0, chunks, step, 0)

    def publish(which, value):
        size, pos, peer, buf, sem = groups[which]
        buf[pos] = value

        def one(s, carry):
            slot = lax.rem(pos + s, size)
            copy(buf.at[pos], buf.at[pos], sem.at[0, s], sem.at[1, pos], peer(slot)).start()
            return carry

        lax.fori_loop(1, size, one, 0)

    def collect(which):
        size, pos, peer, buf, sem = groups[which]

        def one(s, carry):
            slot = lax.rem(pos + s, size)
            pltpu.make_async_copy(buf.at[slot], buf.at[slot], sem.at[1, slot]).wait()
            pltpu.make_async_copy(buf.at[pos], buf.at[pos], sem.at[0, s]).wait()
            return carry

        lax.fori_loop(1, size, one, 0)
        out = buf[0]
        for s in range(1, size):
            out = out + buf[s]
        return out

    by_lane = jnp.sum(jnp.transpose(sink_rows[...]), axis=0, keepdims=True)
    publish(0, jnp.broadcast_to(by_lane, (8, 128)))

    def tail(c, carry):
        relay(2, c - LAG_T1)
        near_lagged(c)
        relay(3, c - LAG_S0)
        return carry

    lax.fori_loop(chunks, chunks + 1, tail, 0)
    publish(1, collect(0))
    lax.fori_loop(chunks + 1, chunks + LAG_LO, tail, 0)
    publish(2, collect(1))

    def ending(c, carry):
        finish(c)
        return carry

    lax.fori_loop(chunks - LAG_END, chunks, ending, 0)
    sg_ref[...] = collect(2)

    def drain(c, carry):
        @pl.when(has_up)
        def _():
            pltpu.make_async_copy(kv1.at[0], kv1.at[0], up_send.at[c]).wait()

        @pl.when(has_up & has_down)
        def _():
            pltpu.make_async_copy(kv1.at[0], kv1.at[0], fw_send.at[c]).wait()

        @pl.when(has_far)
        def _():
            pltpu.make_async_copy(st1.at[0], st1.at[0], t1_send.at[c]).wait()

        @pl.when(has_down)
        def _():
            pltpu.make_async_copy(ss0.at[0], ss0.at[0], s0_send.at[c]).wait()

        @pl.when(is_relay)
        def _():
            for which in range(4):
                pltpu.make_async_copy(kv1.at[0, 0], kv1.at[0, 0], re_send.at[which, c]).wait()

        return carry

    lax.fori_loop(0, chunks, drain, 0)


def solution(mesh):
    n, n_ctx = mesh.shape["dp"], mesh.shape["ctx"]

    def body(queries, key_states, values, out_grad, block_links, sink_logit):
        shape = queries.shape
        tokens, full = shape[1], shape[2]
        heads = sink_logit.shape[0]
        width = full // CHUNKS
        flat = [a.reshape(tokens, full) for a in (queries, key_states, values, out_grad)]
        vmem = pl.BlockSpec(memory_space=pltpu.VMEM)
        smem = pl.BlockSpec(memory_space=pltpu.SMEM)
        wide = pltpu.VMEM((2 * CHUNKS, 2, BLOCK, width), jnp.bfloat16)
        once = pltpu.VMEM((CHUNKS, 2, BLOCK, width), jnp.bfloat16)
        sums = pltpu.VMEM((CHUNKS, 2, BLOCK, width), jnp.float32)
        dma = pltpu.SemaphoreType.DMA
        n_col = 2 * (n_ctx // 8)
        dq, dk, dv, sg = pl.pallas_call(
            functools.partial(body_kernel, (n, n_ctx, heads)),
            out_shape=[jax.ShapeDtypeStruct((tokens, full), jnp.bfloat16)] * 3
            + [jax.ShapeDtypeStruct((8, 128), jnp.float32)],
            in_specs=[smem, smem] + [vmem] * 4,
            out_specs=[vmem] * 4,
            scratch_shapes=[
                wide,
                wide,
                wide,
                wide,
                once,
                once,
                sums,
                sums,
                pltpu.VMEM((128, 128), jnp.float32),
                pltpu.VMEM((8, 8, 128), jnp.float32),
                pltpu.VMEM((n_col, 8, 128), jnp.float32),
                pltpu.VMEM((n // 2, 8, 128), jnp.float32),
                dma((CHUNKS,)),
                dma((2 * CHUNKS,)),
                dma((CHUNKS,)),
                dma((2 * CHUNKS,)),
                dma((CHUNKS,)),
                dma((2 * CHUNKS,)),
                dma((CHUNKS,)),
                dma((2 * CHUNKS,)),
                dma((4, CHUNKS)),
                dma((2, 8)),
                dma((2, n_col)),
                dma((2, n // 2)),
            ],
            compiler_params=pltpu.CompilerParams(
                collective_id=0, has_side_effects=True, vmem_limit_bytes=50 * 1024 * 1024
            ),
        )(block_links, sink_logit, *flat)
        return dq.reshape(shape), dk.reshape(shape), dv.reshape(shape), sg[0, :heads]

    placed = (
        P("ctx", "dp", None),
        P("ctx", "dp", None),
        P("ctx", "dp", None),
        P("ctx", "dp", None),
        P(None, "dp"),
        P(),
    )
    return jax.shard_map(
        body,
        mesh=mesh,
        in_specs=placed,
        out_specs=(P("ctx", "dp", None), P("ctx", "dp", None), P("ctx", "dp", None), P()),
        check_vma=False,
    )
```

```python
import functools

import jax
import jax.numpy as jnp
from jax import lax
from jax.experimental import pallas as pl
from jax.experimental.pallas import tpu as pltpu
from jax.sharding import PartitionSpec as P

MESH = pl.DeviceIdType.MESH
BLOCK = 128
HEAD = 128
CHUNKS = 10
AHEAD = 1
NEG_FILL = -1e30
LAG_LO = 3
LAG_T1 = 2
LAG_S0 = 3
LAG_END = 4


def body_kernel(
    dims,
    links,
    sink,
    q_ref,
    k_ref,
    v_ref,
    g_ref,
    dq_ref,
    dk_ref,
    dv_ref,
    sg_ref,
    kv1,
    kv2,
    rt1,
    rs0,
    st1,
    ss0,
    near,
    own,
    sink_rows,
    plane,
    column,
    row,
    up_send,
    up_recv,
    fw_send,
    fw_recv,
    t1_send,
    t1_recv,
    s0_send,
    s0_recv,
    re_send,
    plane_sem,
    column_sem,
    row_sem,
):
    n, n_ctx, heads = dims
    chunks = CHUNKS
    per = heads // chunks
    width = per * HEAD
    half = n // 2
    scale = HEAD**-0.5
    me = lax.axis_index("dp")
    ctx = lax.axis_index("ctx")
    last = n - 1
    is_lo = me == half - 1
    is_hi = me == half
    is_relay = (me == 0) | (me == last)
    relay_half = jnp.where(me == 0, 1, 0)

    n_plane = 8
    n_zlo = n_ctx // n_plane
    n_col = 2 * n_zlo
    pos_plane = lax.rem(ctx, n_plane)
    zlo = ctx // n_plane
    zhi = me // half
    y = lax.rem(me, half)
    across = lax.rem(zlo + n_zlo // 2, n_zlo) * n_plane + pos_plane
    pos_col = zhi * n_zlo + zlo

    def plane_peer(slot):
        return {"dp": me, "ctx": zlo * n_plane + slot}

    def column_peer(slot):
        return {
            "dp": (slot // n_zlo) * half + y,
            "ctx": lax.rem(slot, n_zlo) * n_plane + pos_plane,
        }

    def row_peer(slot):
        return {"dp": zhi * half + slot, "ctx": ctx}

    groups = (
        (n_plane, pos_plane, plane_peer, plane, plane_sem),
        (n_col, pos_col, column_peer, column, column_sem),
        (half, y, row_peer, row, row_sem),
    )

    barrier = pltpu.get_barrier_semaphore()
    total = 0
    for size, pos, peer, _, _ in groups:

        def greet(step, carry, size=size, pos=pos, peer=peer):
            pl.semaphore_signal(
                barrier, inc=1, device_id=peer(lax.rem(pos + step, size)), device_id_type=MESH
            )
            return carry

        lax.fori_loop(1, size, greet, 0)
        total += size - 1
    is_edge = is_lo | is_hi | is_relay

    @pl.when(is_edge)
    def _():
        facing = jnp.where(me < half, half - 1 - me, half + last - me)
        pl.semaphore_signal(
            barrier, inc=1, device_id={"dp": facing, "ctx": across}, device_id_type=MESH
        )

    pl.semaphore_wait(barrier, total + jnp.where(is_edge, 1, 0))

    def up_device(which):
        relay_dp = last if which == 0 else 0
        return {
            "dp": jnp.where(is_lo, relay_dp, jnp.minimum(me + 1, last)),
            "ctx": jnp.where(is_lo, across, ctx),
        }

    def down_device(which):
        relay_dp = last if which == 0 else 0
        return {
            "dp": jnp.where(is_hi, relay_dp, jnp.maximum(me - 1, 0)),
            "ctx": jnp.where(is_hi, across, ctx),
        }

    def up_slot(c):
        return c + jnp.where(is_lo, chunks, 0)

    def down_slot(c):
        return c + jnp.where(is_hi, chunks, 0)

    def lanes(c):
        return pl.ds(pl.multiple_of(c * width, width), width)

    def copy(src, dst, send, recv, device):
        return pltpu.make_async_remote_copy(
            src_ref=src,
            dst_ref=dst,
            send_sem=send,
            recv_sem=recv,
            device_id=device,
            device_id_type=MESH,
        )

    def own_copies(c):
        slot = up_slot(c)
        return [
            copy(
                ref.at[:, lanes(c)],
                kv1.at[slot, which],
                up_send.at[c],
                up_recv.at[slot],
                up_device(which),
            )
            for which, ref in enumerate((k_ref, v_ref))
        ]

    def send_own(c):
        for each in own_copies(c):
            each.start()

    def pair(src, dst, send, recv, c, slot, device):
        for which in range(2):
            copy(
                src.at[c, which], dst.at[slot, which], send.at[c], recv.at[slot], device(which)
            ).start()

    def send_fw(c):
        pair(kv1, kv2, fw_send, fw_recv, c, up_slot(c), up_device)

    def send_t1(c):
        pair(st1, rt1, t1_send, t1_recv, c, down_slot(c), down_device)

    def send_s0(c):
        pair(ss0, rs0, s0_send, s0_recv, c, down_slot(c), down_device)

    def landed(ref, sem, slot):
        pltpu.make_async_copy(ref.at[slot], ref.at[slot], sem.at[slot]).wait()

    relays = (
        (kv1, up_recv, half),
        (kv2, fw_recv, half),
        (rt1, t1_recv, half - 1),
        (rs0, s0_recv, half - 1),
    )

    def relay(stream, c):
        @pl.when(is_relay & (c >= 0) & (c < chunks))
        def _():
            ref, sem, target = relays[stream]
            held = ref.at[chunks + c, relay_half]
            pltpu.make_async_copy(held, held, sem.at[chunks + c]).wait()
            copy(
                held,
                ref.at[c, relay_half],
                re_send.at[stream, c],
                sem.at[c],
                {"dp": target, "ctx": across},
            ).start()

    has_down = me >= 1
    has_far = me >= 2
    has_up = me <= last - 1

    @pl.when(has_up)
    def _():
        for c in range(AHEAD + 1):
            send_own(jnp.int32(c))

    zero = jnp.zeros((2, BLOCK, width), jnp.bfloat16)

    def clear(ref):
        def one(c, carry):
            ref[c] = zero
            return carry

        lax.fori_loop(0, chunks, one, 0)

    @pl.when(me == 0)
    def _():
        clear(kv1)

    @pl.when(me <= 1)
    def _():
        clear(kv2)

    @pl.when(me == last)
    def _():
        clear(rs0)
        clear(rt1)

    sink_rows[...] = jnp.zeros_like(sink_rows)
    bias = [jnp.where(links[level, 0] >= 0, 0.0, NEG_FILL) for level in range(2)]
    key_pos = lax.broadcasted_iota(jnp.int32, (BLOCK, BLOCK), 0)
    query_pos = lax.broadcasted_iota(jnp.int32, (BLOCK, BLOCK), 1)
    causal = query_pos >= key_pos

    def dot(a, b, dims):
        return lax.dot_general(a, b, (dims, ((), ())), preferred_element_type=jnp.float32)

    def attend(c):
        for i in range(per):
            head = c * per + i
            at = pl.ds(pl.multiple_of(c * width + i * HEAD, HEAD), HEAD)
            part = slice(i * HEAD, (i + 1) * HEAD)
            q = q_ref[:, at]
            g = g_ref[:, at]
            keys = (k_ref[:, at], kv1[c, 0, :, part], kv2[c, 0, :, part])
            vals = (v_ref[:, at], kv1[c, 1, :, part], kv2[c, 1, :, part])
            logit = sink[head]
            scores = [dot(k, q, ((1,), (1,))) * scale for k in keys]
            scores = [
                jnp.where(causal, scores[0], NEG_FILL),
                scores[1] + bias[0],
                scores[2] + bias[1],
            ]
            top = jnp.maximum(jnp.maximum(scores[0], scores[1]), scores[2])
            top = jnp.maximum(jnp.max(top, axis=0, keepdims=True), logit)
            exps = [jnp.exp(s - top) for s in scores]
            sink_exp = jnp.exp(logit - top)
            denom = jnp.sum(exps[0] + exps[1] + exps[2], axis=0, keepdims=True) + sink_exp
            inverse = 1.0 / denom
            probs = [e * inverse for e in exps]
            prob_grads = [dot(v, g, ((1,), (1,))) for v in vals]
            mixed = (
                probs[0] * prob_grads[0] + probs[1] * prob_grads[1] + probs[2] * prob_grads[2]
            )
            delta = jnp.sum(mixed, axis=0, keepdims=True)
            score_grads = [
                (p * (d - delta)).astype(jnp.bfloat16) for p, d in zip(probs, prob_grads)
            ]
            weights = [p.astype(jnp.bfloat16) for p in probs]
            sink_rows[pl.ds(head, 1), :] = -(sink_exp * inverse * delta)
            dq = dot(score_grads[0], keys[0], ((0,), (0,)))
            dq += dot(score_grads[1], keys[1], ((0,), (0,)))
            dq += dot(score_grads[2], keys[2], ((0,), (0,)))
            dq_ref[:, at] = (dq * scale).astype(jnp.bfloat16)
            own[c, 0, :, part] = dot(score_grads[0], q, ((1,), (0,))) * scale
            own[c, 1, :, part] = dot(weights[0], g, ((1,), (0,)))
            near[c, 0, :, part] = dot(score_grads[1], q, ((1,), (0,))) * scale
            near[c, 1, :, part] = dot(weights[1], g, ((1,), (0,)))
            st1[c, 0, :, part] = (dot(score_grads[2], q, ((1,), (0,))) * scale).astype(
                jnp.bfloat16
            )
            st1[c, 1, :, part] = dot(weights[2], g, ((1,), (0,))).astype(jnp.bfloat16)

    def pass_near(c):
        @pl.when(has_down & has_up)
        def _():
            landed(rt1, t1_recv, c)

        @pl.when(has_down)
        def _():
            ss0[c] = (near[c] + rt1[c].astype(jnp.float32)).astype(jnp.bfloat16)
            send_s0(c)

    def finish(c):
        @pl.when(has_up)
        def _():
            landed(rs0, s0_recv, c)

        dk_ref[:, lanes(c)] = (own[c, 0] + rs0[c, 0].astype(jnp.float32)).astype(jnp.bfloat16)
        dv_ref[:, lanes(c)] = (own[c, 1] + rs0[c, 1].astype(jnp.float32)).astype(jnp.bfloat16)

    def forward(c):
        @pl.when(has_down & (c < chunks))
        def _():
            landed(kv1, up_recv, c)

        @pl.when(has_down & has_up & (c < chunks))
        def _():
            send_fw(c)

    lag = jnp.where(is_lo, LAG_LO, 1)

    def near_lagged(c):
        @pl.when((c >= lag) & (c - lag < chunks))
        def _():
            pass_near(c - lag)

    def step(c, carry):
        relay(0, c + 1)
        forward(c + 1)

        @pl.when(has_up & (c + AHEAD + 1 < chunks))
        def _():
            send_own(c + AHEAD + 1)

        relay(1, c)

        @pl.when(has_far)
        def _():
            landed(kv2, fw_recv, c)

        attend(c)

        @pl.when(has_far)
        def _():
            send_t1(c)

        relay(2, c - LAG_T1)
        near_lagged(c)
        relay(3, c - LAG_S0)

        @pl.when(c >= LAG_END)
        def _():
            finish(c - LAG_END)

        return carry

    relay(0, jnp.int32(0))
    forward(jnp.int32(0))
    lax.fori_loop(0, chunks, step, 0)

    def publish(which, value):
        size, pos, peer, buf, sem = groups[which]
        buf[pos] = value

        def one(s, carry):
            slot = lax.rem(pos + s, size)
            copy(buf.at[pos], buf.at[pos], sem.at[0, s], sem.at[1, pos], peer(slot)).start()
            return carry

        lax.fori_loop(1, size, one, 0)

    def collect(which):
        size, pos, peer, buf, sem = groups[which]

        def one(s, carry):
            slot = lax.rem(pos + s, size)
            pltpu.make_async_copy(buf.at[slot], buf.at[slot], sem.at[1, slot]).wait()
            pltpu.make_async_copy(buf.at[pos], buf.at[pos], sem.at[0, s]).wait()
            return carry

        lax.fori_loop(1, size, one, 0)
        out = buf[0]
        for s in range(1, size):
            out = out + buf[s]
        return out

    by_lane = jnp.sum(jnp.transpose(sink_rows[...]), axis=0, keepdims=True)
    publish(0, jnp.broadcast_to(by_lane, (8, 128)))

    def tail(c, carry):
        relay(2, c - LAG_T1)
        near_lagged(c)
        relay(3, c - LAG_S0)
        return carry

    lax.fori_loop(chunks, chunks + 1, tail, 0)
    publish(1, collect(0))
    lax.fori_loop(chunks + 1, chunks + LAG_LO, tail, 0)
    publish(2, collect(1))

    def ending(c, carry):
        finish(c)
        return carry

    lax.fori_loop(chunks - LAG_END, chunks, ending, 0)
    sg_ref[...] = collect(2)

    def drain(c, carry):
        @pl.when(has_up)
        def _():
            pltpu.make_async_copy(kv1.at[0], kv1.at[0], up_send.at[c]).wait()

        @pl.when(has_up & has_down)
        def _():
            pltpu.make_async_copy(kv1.at[0], kv1.at[0], fw_send.at[c]).wait()

        @pl.when(has_far)
        def _():
            pltpu.make_async_copy(st1.at[0], st1.at[0], t1_send.at[c]).wait()

        @pl.when(has_down)
        def _():
            pltpu.make_async_copy(ss0.at[0], ss0.at[0], s0_send.at[c]).wait()

        @pl.when(is_relay)
        def _():
            for which in range(4):
                pltpu.make_async_copy(kv1.at[0, 0], kv1.at[0, 0], re_send.at[which, c]).wait()

        return carry

    lax.fori_loop(0, chunks, drain, 0)


def solution(mesh):
    n, n_ctx = mesh.shape["dp"], mesh.shape["ctx"]

    def body(queries, key_states, values, out_grad, block_links, sink_logit):
        shape = queries.shape
        tokens, full = shape[1], shape[2]
        heads = sink_logit.shape[0]
        width = full // CHUNKS
        flat = [a.reshape(tokens, full) for a in (queries, key_states, values, out_grad)]
        vmem = pl.BlockSpec(memory_space=pltpu.VMEM)
        smem = pl.BlockSpec(memory_space=pltpu.SMEM)
        wide = pltpu.VMEM((2 * CHUNKS, 2, BLOCK, width), jnp.bfloat16)
        once = pltpu.VMEM((CHUNKS, 2, BLOCK, width), jnp.bfloat16)
        sums = pltpu.VMEM((CHUNKS, 2, BLOCK, width), jnp.float32)
        dma = pltpu.SemaphoreType.DMA
        n_col = 2 * (n_ctx // 8)
        dq, dk, dv, sg = pl.pallas_call(
            functools.partial(body_kernel, (n, n_ctx, heads)),
            out_shape=[jax.ShapeDtypeStruct((tokens, full), jnp.bfloat16)] * 3
            + [jax.ShapeDtypeStruct((8, 128), jnp.float32)],
            in_specs=[smem, smem] + [vmem] * 4,
            out_specs=[vmem] * 4,
            scratch_shapes=[
                wide,
                wide,
                wide,
                wide,
                once,
                once,
                sums,
                sums,
                pltpu.VMEM((128, 128), jnp.float32),
                pltpu.VMEM((8, 8, 128), jnp.float32),
                pltpu.VMEM((n_col, 8, 128), jnp.float32),
                pltpu.VMEM((n // 2, 8, 128), jnp.float32),
                dma((CHUNKS,)),
                dma((2 * CHUNKS,)),
                dma((CHUNKS,)),
                dma((2 * CHUNKS,)),
                dma((CHUNKS,)),
                dma((2 * CHUNKS,)),
                dma((CHUNKS,)),
                dma((2 * CHUNKS,)),
                dma((4, CHUNKS)),
                dma((2, 8)),
                dma((2, n_col)),
                dma((2, n // 2)),
            ],
            compiler_params=pltpu.CompilerParams(
                collective_id=0, has_side_effects=True, vmem_limit_bytes=50 * 1024 * 1024
            ),
        )(block_links, sink_logit, *flat)
        return dq.reshape(shape), dk.reshape(shape), dv.reshape(shape), sg[0, :heads]

    placed = (
        P("ctx", "dp", None),
        P("ctx", "dp", None),
        P("ctx", "dp", None),
        P("ctx", "dp", None),
        P(None, "dp"),
        P(),
    )
    return jax.shard_map(
        body,
        mesh=mesh,
        in_specs=placed,
        out_specs=(P("ctx", "dp", None), P("ctx", "dp", None), P("ctx", "dp", None), P()),
        check_vma=False,
    )
```
